32 devices in a mesh: fsdp: 8 (over z, y), tp: 4 (over x, core).
Axes of the slice: x: 2, y: 2, z: 4, core: 2. Of those that a mesh axis runs over, the one named last changes fastest.
Arguments:
- grads: bfloat16 [8, 2, 4096, 2048], P('fsdp', None, 'tp'), may hold values from -144 to 144
- master: float32 [4096, 2048], P('tp', 'fsdp'), may hold values from -0.3125 to 0.3125
- moment: float32 [4096, 2048], P('tp', 'fsdp'), may hold values from -1.5 to 1.5
- second: float32 [4096, 2048], P('tp', 'fsdp'), may hold values from 0.02 to 0.3
- stats: float32 [4, 1024, 1024], P('tp', 'fsdp'), may hold values from -0.05 to 0.35
- basis: float32 [4, 1024, 1024], P('tp', 'fsdp'), may hold values from -0.5 to 1.5
Outputs:
- weights: bfloat16 [4096, 2048], P('tp')
- master_new: float32 [4096, 2048], P('tp', 'fsdp')
- moment_new: float32 [4096, 2048], P('tp', 'fsdp')
- second_new: float32 [4096, 2048], P('tp', 'fsdp')
- stats_new: float32 [4, 1024, 1024], P('tp', 'fsdp')
- basis_new: float32 [4, 1024, 1024], P('tp', 'fsdp')
The draws below stay inside these ranges and needn't reach their ends.
All inputs are finite; a program needn't handle non-finite values.
Results may differ from the reference program's by a relative error of at most 0.007.
Values may be sent and summed in bfloat16 or wider, within the bound.
A program may use at most 128 MiB of HBM per device.

```python
import math
import jax
import jax.numpy as jnp
from jax import lax

D = 4096
KVW = 2048
BS = 1024
MB = 2
NSK = 2
NBLK = 4
NREP = 8


def draw_grads(key, part):
    noise_key = jax.random.fold_in(key, 5)
    pair_key = jax.random.fold_in(key, 7)
    row_pos = jnp.arange(D).astype(jnp.float32) / float(D - 1)
    col_pos = jnp.arange(KVW).astype(jnp.float32) / float(KVW - 1)
    row_scale = jnp.exp(math.log(2.0) * row_pos)
    pairing = jax.random.permutation(pair_key, NREP)
    col_block = jnp.arange(KVW) // (KVW // NREP)
    spike = jnp.where(col_block[None, :] == pairing[:, None], 4.0, 1.0).astype(jnp.float32)
    noise = jnp.clip(jax.random.normal(noise_key, (NREP, MB, D, KVW), jnp.float32), -6.0, 6.0)
    col_scale = jnp.exp(math.log(3.0) * col_pos)
    return (noise * spike[:, None, None, :] * row_scale[None, None, :, None] * col_scale[None, None, None, :]).astype(jnp.bfloat16)


def draw_basis(key, part):
    identity = (jnp.arange(BS)[:, None] == jnp.arange(BS)[None, :]).astype(jnp.float32)
    noise = jax.random.normal(key, (NBLK, BS, BS), jnp.float32)
    return identity[None] + noise * (0.5 / math.sqrt(BS))


def draw_stats(key, part):
    identity = (jnp.arange(BS)[:, None] == jnp.arange(BS)[None, :]).astype(jnp.float32)
    first_key = jax.random.fold_in(key, 11)
    second_key = jax.random.fold_in(key, 23)
    levels = jax.random.uniform(first_key, (NBLK, BS), jnp.float32, math.log(0.02), math.log(0.2))
    noise = jax.random.normal(second_key, (NBLK, BS, BS), jnp.float32)
    symmetric = (noise + jnp.swapaxes(noise, 1, 2)) * (0.002 / math.sqrt(2.0))
    return identity[None] * jnp.exp(levels)[:, :, None] + symmetric * (1.0 - identity[None])


def shard_levels(rng, extent, pieces, least, top_value):
    factor_of, own = 1.0, jax.random.fold_in(rng, 6)
    for position, parts in pieces:
        steps = jnp.exp(jax.random.uniform(jax.random.fold_in(own, position), (parts,), jnp.float32, least / len(pieces), top_value / len(pieces)))
        factor_of = factor_of * jnp.repeat(steps, extent[position] // parts).reshape([-1 if axis == position else 1 for axis in range(len(extent))])
    return factor_of


def bell_draw(key, shape, scale, reach, shards=(), dtype=jnp.bfloat16):
    entries = scale * jax.random.normal(key, shape, jnp.float32)
    if shards:
        entries = entries * shard_levels(key, shape, shards, -0.22, 0.18)
    return jnp.clip(entries, -reach, reach).astype(dtype)


def setup_inputs(seed: int = 0) -> dict:
    keys = jax.random.split(jax.random.key(seed), 7)
    grads = draw_grads(jax.random.fold_in(keys[6], 71), 0)
    master = bell_draw(keys[1], (D, KVW), 0.02, 0.3125, ((0, 4), (1, 8)), jnp.float32)
    moment = bell_draw(keys[2], (D, KVW), 0.1, 1.5, ((0, 4), (1, 8)), jnp.float32)
    second = jnp.clip(jnp.exp(math.log(0.3) - 2.7080503 * jax.random.uniform(keys[3], (D, KVW), jnp.float32) ** shard_levels(keys[3], (D, KVW), ((0, 4), (1, 8)), -0.2, 0.2)), 0.02, 0.3)
    stats = draw_stats(jax.random.fold_in(keys[6], 71), 0)
    basis = draw_basis(jax.random.fold_in(keys[6], 71), 0)
    return dict(grads=grads, master=master, moment=moment, second=second, stats=stats, basis=basis)


poly_first = 3.4445
poly_second = -4.775
poly_third = 2.0315

def reference(grads, master, moment, second, stats, basis):
    high = lax.Precision.HIGHEST

    def accumulate(carry, replica):
        return (carry + lax.optimization_barrier(jnp.sum(replica.astype(jnp.float32), axis=0)), None)
    total, unused = lax.scan(accumulate, jnp.zeros((D, KVW), jnp.float32), grads)
    factor = jnp.minimum(1.0, jnp.sqrt(float(D * KVW) / (jnp.sum(total * total) + 1e-06)))
    clipped = (total * factor).reshape(NBLK, BS, KVW)
    rotated = jnp.einsum('bkr,bkc->brc', basis, clipped, precision=high).reshape(D, KVW)
    moment_new = 0.9 * moment + 0.1 * rotated
    second_new = 0.95 * second + 0.05 * rotated * rotated
    update = (moment_new / (jnp.sqrt(second_new) + 1e-08)).reshape(NBLK, BS, KVW)
    delta = jnp.einsum('brk,bkc->brc', basis, update, precision=high).reshape(D, KVW)
    master_new = master - 0.01 * (delta + 0.1 * master)
    weights = master_new.astype(jnp.bfloat16)
    outer = jnp.einsum('brc,bkc->brk', clipped, clipped, precision=high)
    stats_new = 0.9 * stats + 0.1 / KVW * outer
    power = jnp.einsum('brk,bkc->brc', stats_new, basis, precision=high)
    squares = lax.optimization_barrier(jnp.sum(power * power, axis=(1, 2), keepdims=True))
    current = power / jnp.sqrt(squares + 1e-06)
    for step in range(NSK):
        gram = jnp.einsum('bkr,bkc->brc', current, current, precision=high)
        product = jnp.einsum('brk,bkc->brc', current, gram, precision=high)
        second_term = jnp.einsum('brk,bkc->brc', product, gram, precision=high)
        current = poly_first * current + poly_second * product + poly_third * second_term
    return (weights, master_new, moment_new, second_new, stats_new, current)
```

```python
import jax
import jax.numpy as jnp
from jax import lax
from jax.sharding import PartitionSpec as P

D = 4096
KVW = 2048

poly_first = 3.4445
poly_second = -4.775
poly_third = 2.0315
bf16 = jnp.bfloat16
f32 = jnp.float32


def exact(a, b):
    return jnp.dot(a, b, precision=lax.Precision.HIGHEST)


def split(a):
    top = a.astype(bf16)
    return top, (a - top.astype(f32)).astype(bf16)


def three(a, b):
    a_top, a_low = split(a)
    b_top, b_low = split(b)
    mm = lambda u, v: jnp.dot(u, v, preferred_element_type=f32)
    return mm(a_top, b_top) + (mm(a_low, b_top) + mm(a_top, b_low))


def body(grads, master, moment, second, stats, basis):
    n = lax.axis_size("fsdp")
    rows = master.shape[0]
    cols = master.shape[1]
    own_rows = basis[0]
    stat_rows = stats[0]
    whole = lax.all_gather(own_rows.astype(bf16), "fsdp", axis=0, tiled=True)
    local = jnp.sum(grads.astype(f32), axis=(0, 1)).astype(bf16)
    pieces = lax.all_to_all(local, "fsdp", split_axis=1, concat_axis=0, tiled=True)
    summed = jnp.sum(pieces.reshape(n, rows, cols).astype(f32), axis=0)
    squares = jnp.sum(lax.all_gather(jnp.sum(summed * summed).reshape(1), ("fsdp", "tp")))
    ratio = jnp.minimum(1.0, jnp.sqrt(float(D * KVW) / (squares + 1e-06)))
    total = summed.astype(bf16)
    part = jnp.dot(total, total.T, preferred_element_type=f32).astype(bf16)
    strips = lax.all_to_all(part, "fsdp", split_axis=0, concat_axis=0, tiled=True)
    outer = jnp.sum(strips.reshape(n, rows // n, rows).astype(f32), axis=0) * (ratio * ratio)
    stats_new = 0.9 * stat_rows + 0.1 / KVW * outer
    s_top, s_low = split(stats_new)
    power = jnp.dot(s_top, whole, preferred_element_type=f32) + jnp.dot(s_low, whole, preferred_element_type=f32)
    every = lax.all_gather(power.astype(bf16), "fsdp", axis=0, tiled=True)
    rotated = jnp.dot(whole.T, total, preferred_element_type=f32) * ratio
    moment_new = 0.9 * moment + 0.1 * rotated
    second_new = 0.95 * second + 0.05 * rotated * rotated
    update = moment_new / (jnp.sqrt(second_new) + 1e-08)
    delta = jnp.dot(whole, update.astype(bf16), preferred_element_type=f32)
    master_new = master - 0.01 * (delta + 0.1 * master)
    weights = lax.all_gather(master_new.astype(bf16), "fsdp", axis=1, tiled=True)
    raw = jnp.dot(every.T, every, preferred_element_type=f32)
    diag = lax.broadcasted_iota(jnp.int32, (rows, rows), 0) == lax.broadcasted_iota(jnp.int32, (rows, rows), 1)
    norm = 1.0 / jnp.sqrt(jnp.sum(jnp.where(diag, raw, 0.0)) + 1e-06)
    gram = raw * (norm * norm)
    current = power * norm
    mixed = jnp.where(diag, poly_first, 0.0) + poly_second * gram + poly_third * three(gram, gram)
    current = three(current, mixed)
    gram = three(mixed, three(mixed, gram))
    product = three(current, gram)
    current = poly_first * current + poly_second * product + poly_third * three(product, gram)
    return (weights, master_new, moment_new, second_new, stats_new[None], current[None])


def solution(mesh):
    in_specs = (
        P("fsdp", None, "tp", None),
        P("tp", "fsdp"),
        P("tp", "fsdp"),
        P("tp", "fsdp"),
        P("tp", "fsdp", None),
        P("tp", "fsdp", None),
    )
    out_specs = (
        P("tp", None),
        P("tp", "fsdp"),
        P("tp", "fsdp"),
        P("tp", "fsdp"),
        P("tp", "fsdp", None),
        P("tp", "fsdp", None),
    )
    return jax.shard_map(body, mesh=mesh, in_specs=in_specs, out_specs=out_specs, check_vma=False)
```

```python
import functools

import jax
import jax.numpy as jnp
from jax import lax
from jax.experimental import pallas as pl
from jax.experimental.pallas import tpu as pltpu
from jax.sharding import PartitionSpec as P

D = 4096
KVW = 2048

poly_first = 3.4445
poly_second = -4.775
poly_third = 2.0315
bf16 = jnp.bfloat16
f32 = jnp.float32
MESH = pl.DeviceIdType.MESH
VMEM_BYTES = 40 * 1024 * 1024


def mm(a, b):
    return jnp.dot(a.astype(bf16), b.astype(bf16), preferred_element_type=f32)


def greet(n, tp_peers):
    me = lax.axis_index("fsdp")
    barrier = pltpu.get_barrier_semaphore()
    for step in range(1, n):
        pl.semaphore_signal(barrier, inc=1, device_id={"fsdp": lax.rem(me + step, n)}, device_id_type=MESH)
    if tp_peers > 1:
        lane = lax.axis_index("tp")
        for step in range(1, tp_peers):
            pl.semaphore_signal(barrier, inc=1, device_id={"tp": lax.rem(lane + step, tp_peers)}, device_id_type=MESH)
    pl.semaphore_wait(barrier, n - 1 + tp_peers - 1)


def remote(src, dst, send_sem, recv_sem, target, axis="fsdp"):
    return pltpu.make_async_remote_copy(
        src_ref=src, dst_ref=dst, send_sem=send_sem, recv_sem=recv_sem,
        device_id={axis: target}, device_id_type=MESH,
    )


def exchange(n, produce, finish, out1, in1, out2, in2, s1, r1, s2, r2):
    half = n // 2
    me = lax.axis_index("fsdp")
    side = lax.rem(me, 2)
    pair = me // 2
    mate = me + 1 - 2 * side
    groups = [lax.rem(pair + 1 + k, half) for k in range(half)]
    first = [remote(out1.at[k], in1.at[k], s1.at[k], r1.at[k], mate) for k in range(half)]
    second = [remote(out2.at[k], in2.at[k], s2.at[k], r2.at[k], 2 * groups[k] + side) for k in range(half - 1)]

    def start(k):
        produce(2 * groups[k] + 1 - side, 2 * k, None, out1.at[k])
        first[k].start()

    for k in range(min(2, half)):
        start(k)
    for k in range(half):
        first[k].wait_recv()
        if k + 2 < half:
            start(k + 2)
        if k < half - 1:
            produce(2 * groups[k] + side, 2 * k + 1, in1.at[k], out2.at[k])
            second[k].start()
    for k in range(half - 1):
        second[k].wait_recv()
    finish(me, 2 * half - 1, in1.at[half - 1], in2)
    for k in range(half):
        first[k].wait_send()
    for k in range(half - 1):
        second[k].wait_send()


def grads_kernel(n, lanes, grads, total, squares, held, out1, in1, out2, in2, own_sq, in_sq, lane_sq, in_lane,
                 loads, s1, r1, s2, r2, sq_s, sq_r, lane_s, lane_r):
    half = n // 2
    rows, cols = total.shape
    micro = held.shape[1]
    tile = 128
    me = lax.axis_index("fsdp")
    side = lax.rem(me, 2)
    pair = me // 2
    copies = []
    for k in range(half):
        group = lax.rem(pair + 1 + k, half)
        for which, chunk in ((0, 2 * group + 1 - side), (1, 2 * group + side)):
            start = pl.multiple_of(chunk * cols, 128)
            copies.append(pltpu.make_async_copy(
                grads.at[0, :, :, pl.ds(start, cols)], held.at[2 * k + which], loads.at[2 * k + which]))
    order = [0, 2] if half > 1 else [0]
    order += [i for i in range(n) if i not in order]
    for i in order:
        copies[i].start()
    greet(n, lanes)

    def local(slot, at):
        value = held[slot, 0, at, :].astype(f32)
        for index in range(1, micro):
            value = value + held[slot, index, at, :].astype(f32)
        return value

    def produce(chunk, slot, add, out):
        copies[slot].wait()

        def step(i, carry):
            at = pl.ds(pl.multiple_of(i * tile, tile), tile)
            value = local(slot, at)
            if add is not None:
                value = value + add[at, :].astype(f32)
            out[at, :] = value.astype(bf16)
            return carry

        lax.fori_loop(0, rows // tile, step, 0)

    def finish(chunk, slot, add, others):
        copies[slot].wait()

        def step(i, carry):
            at = pl.ds(pl.multiple_of(i * tile, tile), tile)
            value = local(slot, at) + add[at, :].astype(f32)
            for k in range(half - 1):
                value = value + others[k, at, :].astype(f32)
            total[at, :] = value.astype(bf16)
            return carry + jnp.sum((value * value).reshape(tile // 8, 8, cols), axis=0)

        sums = lax.fori_loop(0, rows // tile, step, jnp.zeros((8, cols), f32))
        part = sums[:, :128]
        for c in range(1, cols // 128):
            part = part + sums[:, c * 128 : (c + 1) * 128]
        own_sq[...] = part

    exchange(n, produce, finish, out1, in1, out2, in2, s1, r1, s2, r2)
    sends = [remote(own_sq, in_sq.at[k], sq_s.at[k], sq_r.at[k], lax.rem(me + 1 + k, n)) for k in range(n - 1)]
    for send in sends:
        send.start()
    value = own_sq[...]
    for k, send in enumerate(sends):
        send.wait()
        value = value + in_sq[k]
    lane_sq[...] = value
    lane = lax.axis_index("tp")
    sends = [remote(lane_sq, in_lane.at[k], lane_s.at[k], lane_r.at[k], lax.rem(lane + 1 + k, lanes), "tp")
             for k in range(lanes - 1)]
    for send in sends:
        send.start()
    for k, send in enumerate(sends):
        send.wait()
        value = value + in_lane[k]
    squares[...] = value


def sum_grads(grads, n, lanes):
    unused, micro, rows, width = grads.shape
    cols = width // n
    half = n // 2
    dma = pltpu.SemaphoreType.DMA
    piece = pltpu.VMEM((half, rows, cols), bf16)
    small = max(half - 1, 1)
    other = pltpu.VMEM((small, rows, cols), bf16)
    return pl.pallas_call(
        functools.partial(grads_kernel, n, lanes),
        out_shape=(jax.ShapeDtypeStruct((rows, cols), bf16), jax.ShapeDtypeStruct((8, 128), f32)),
        in_specs=[pl.BlockSpec(memory_space=pl.ANY)],
        out_specs=(pl.BlockSpec(memory_space=pltpu.VMEM), pl.BlockSpec(memory_space=pltpu.VMEM)),
        scratch_shapes=[
            pltpu.VMEM((n, micro, rows, cols), bf16), piece, piece, other, other,
            pltpu.VMEM((8, 128), f32), pltpu.VMEM((n - 1, 8, 128), f32),
            pltpu.VMEM((8, 128), f32), pltpu.VMEM((max(lanes - 1, 1), 8, 128), f32),
            dma((n,)), dma((half,)), dma((half,)), dma((small,)), dma((small,)),
            dma((n - 1,)), dma((n - 1,)), dma((max(lanes - 1, 1),)), dma((max(lanes - 1, 1),)),
        ],
        compiler_params=pltpu.CompilerParams(collective_id=0, has_side_effects=True, vmem_limit_bytes=VMEM_BYTES),
    )(grads)


def outer_kernel(n, total, outer, out1, in1, out2, in2, s1, r1, s2, r2):
    half = n // 2
    strip = outer.shape[0]
    greet(n, 1)

    def local(chunk):
        at = pl.ds(pl.multiple_of(chunk * strip, strip), strip)
        return lax.dot_general(total[at, :], total[...], (((1,), (1,)), ((), ())), preferred_element_type=f32)

    def produce(chunk, slot, add, out):
        value = local(chunk)
        if add is not None:
            value = value + add[...].astype(f32)
        out[...] = value.astype(bf16)

    def finish(chunk, slot, add, others):
        value = local(chunk) + add[...].astype(f32)
        for k in range(half - 1):
            value = value + others[k].astype(f32)
        outer[...] = value

    exchange(n, produce, finish, out1, in1, out2, in2, s1, r1, s2, r2)


def sum_outer(total, n):
    rows = total.shape[0]
    strip = rows // n
    half = n // 2
    small = max(half - 1, 1)
    dma = pltpu.SemaphoreType.DMA
    piece = pltpu.VMEM((half, strip, rows), bf16)
    other = pltpu.VMEM((small, strip, rows), bf16)
    return pl.pallas_call(
        functools.partial(outer_kernel, n),
        out_shape=jax.ShapeDtypeStruct((strip, rows), f32),
        in_specs=[pl.BlockSpec(memory_space=pltpu.VMEM)],
        out_specs=pl.BlockSpec(memory_space=pltpu.VMEM),
        scratch_shapes=[piece, piece, other, other, dma((half,)), dma((half,)), dma((small,)), dma((small,))],
        compiler_params=pltpu.CompilerParams(collective_id=1, has_side_effects=True, vmem_limit_bytes=VMEM_BYTES),
    )(total)


def gather_kernel(n, own, every, s1, r1, s2, r2):
    half = n // 2
    me = lax.axis_index("fsdp")
    side = lax.rem(me, 2)
    pair = me // 2
    mate = me + 1 - 2 * side
    greet(n, 1)
    across = [remote(own, every.at[me], s2.at[k], r2.at[k], 2 * lax.rem(pair + 1 + k, half) + side)
              for k in range(half - 1)]
    for copy in across:
        copy.start()
    near = [remote(own, every.at[me], s1.at[0], r1.at[0], mate)]
    near[0].start()
    every[me] = own[...]
    for k in range(half - 1):
        across[k].wait_recv()
        source = 2 * lax.rem(pair + half - 1 - k, half) + side
        near.append(remote(every.at[source], every.at[source], s1.at[k + 1], r1.at[k + 1], mate))
        near[-1].start()
    for copy in near:
        copy.wait()
    for copy in across:
        copy.wait_send()


def gather_rows(own, n, key):
    strip, width = own.shape
    half = n // 2
    small = max(half - 1, 1)
    dma = pltpu.SemaphoreType.DMA
    every = pl.pallas_call(
        functools.partial(gather_kernel, n),
        out_shape=jax.ShapeDtypeStruct((n, strip, width), own.dtype),
        in_specs=[pl.BlockSpec(memory_space=pltpu.VMEM)],
        out_specs=pl.BlockSpec(memory_space=pltpu.VMEM),
        scratch_shapes=[dma((half,)), dma((half,)), dma((small,)), dma((small,))],
        compiler_params=pltpu.CompilerParams(collective_id=key, has_side_effects=True, vmem_limit_bytes=VMEM_BYTES),
    )(own)
    return every.reshape(n * strip, width)


def plain_grads(grads, n, lanes):
    rows = grads.shape[2]
    local = jnp.sum(grads.astype(f32), axis=(0, 1)).astype(bf16)
    pieces = lax.all_to_all(local, "fsdp", split_axis=1, concat_axis=0, tiled=True)
    summed = jnp.sum(pieces.reshape(n, rows, -1).astype(f32), axis=0)
    squares = lax.psum(jnp.sum(summed * summed), ("fsdp", "tp"))
    return summed.astype(bf16), squares


def body(n, lanes, grads, master, moment, second, stats, basis):
    rows, cols = master.shape
    own_rows = basis[0]
    stat_rows = stats[0]
    whole = lax.all_gather(own_rows.astype(bf16), "fsdp", axis=0, tiled=True)
    if cols % 128 == 0 and n % 2 == 0:
        total, squares = sum_grads(grads, n, lanes)
    else:
        total, squares = plain_grads(grads, n, lanes)
    ratio = jnp.minimum(1.0, jnp.sqrt(float(D * KVW) / (jnp.sum(squares) + 1e-06)))
    rotated = mm(whole.T, total) * ratio
    moment_new = 0.9 * moment + 0.1 * rotated
    second_new = 0.95 * second + 0.05 * rotated * rotated
    update = moment_new / (jnp.sqrt(second_new) + 1e-08)
    delta = mm(whole, update)
    master_new = master - 0.01 * (delta + 0.1 * master)
    weights = lax.all_gather(master_new.astype(bf16), "fsdp", axis=1, tiled=True)
    outer = sum_outer(total, n) * (ratio * ratio)
    stats_new = 0.9 * stat_rows + 0.1 / KVW * outer
    top = stats_new.astype(bf16)
    power = mm(top, whole) + mm(stats_new - top.astype(f32), whole)
    every = gather_rows(power.astype(bf16), n, 2)
    raw = mm(every.T, every)
    norm = 1.0 / jnp.sqrt(jnp.sum(jnp.square(every.astype(f32))) + 1e-06)
    gram = raw * (norm * norm)
    current = power * norm
    bend = poly_second * gram + poly_third * mm(gram, gram)
    current = poly_first * current + mm(current, bend)
    once = poly_first * gram + mm(bend, gram)
    gram = poly_first * once + mm(bend, once)
    product = mm(current, gram)
    current = poly_first * current + poly_second * product + poly_third * mm(product, gram)
    return (weights, master_new, moment_new, second_new, stats_new[None], current[None])


def solution(mesh):
    in_specs = (
        P("fsdp", None, "tp", None),
        P("tp", "fsdp"),
        P("tp", "fsdp"),
        P("tp", "fsdp"),
        P("tp", "fsdp", None),
        P("tp", "fsdp", None),
    )
    out_specs = (
        P("tp", None),
        P("tp", "fsdp"),
        P("tp", "fsdp"),
        P("tp", "fsdp"),
        P("tp", "fsdp", None),
        P("tp", "fsdp", None),
    )
    step = functools.partial(body, mesh.shape["fsdp"], mesh.shape["tp"])
    return jax.shard_map(step, mesh=mesh, in_specs=in_specs, out_specs=out_specs, check_vma=False)
```

```python
import functools

import jax
import jax.numpy as jnp
from jax import lax
from jax.experimental import pallas as pl
from jax.experimental.pallas import tpu as pltpu
from jax.sharding import PartitionSpec as P

D = 4096
KVW = 2048

poly_first = 3.4445
poly_second = -4.775
poly_third = 2.0315
bf16 = jnp.bfloat16
f32 = jnp.float32
MESH = pl.DeviceIdType.MESH
VMEM_BYTES = 40 * 1024 * 1024


def mm(a, b):
    return jnp.dot(a.astype(bf16), b.astype(bf16), preferred_element_type=f32)


def greet(n, tp_peers):
    me = lax.axis_index("fsdp")
    barrier = pltpu.get_barrier_semaphore()
    for step in range(1, n):
        pl.semaphore_signal(barrier, inc=1, device_id={"fsdp": lax.rem(me + step, n)}, device_id_type=MESH)
    if tp_peers > 1:
        lane = lax.axis_index("tp")
        for step in range(1, tp_peers):
            pl.semaphore_signal(barrier, inc=1, device_id={"tp": lax.rem(lane + step, tp_peers)}, device_id_type=MESH)
    pl.semaphore_wait(barrier, n - 1 + tp_peers - 1)


def remote(src, dst, send_sem, recv_sem, target, axis="fsdp"):
    return pltpu.make_async_remote_copy(
        src_ref=src, dst_ref=dst, send_sem=send_sem, recv_sem=recv_sem,
        device_id={axis: target}, device_id_type=MESH,
    )


def exchange(n, produce, finish, out1, in1, out2, in2, s1, r1, s2, r2, beside=None):
    half = n // 2
    me = lax.axis_index("fsdp")
    side = lax.rem(me, 2)
    pair = me // 2
    mate = me + 1 - 2 * side
    groups = [lax.rem(pair + 1 + k, half) for k in range(half)]
    first = [remote(out1.at[k], in1.at[k], s1.at[k], r1.at[k], mate) for k in range(half)]
    second = [remote(out2.at[k], in2.at[k], s2.at[k], r2.at[k], 2 * groups[k] + side) for k in range(half - 1)]

    def start(k):
        produce(2 * groups[k] + 1 - side, 2 * k, None, out1.at[k])
        first[k].start()

    for k in range(min(2, half)):
        start(k)
    for k in range(half):
        first[k].wait_recv()
        if k + 2 < half:
            start(k + 2)
        if k < half - 1:
            produce(2 * groups[k] + side, 2 * k + 1, in1.at[k], out2.at[k])
            second[k].start()
        if beside is not None:
            beside(k)
    for k in range(half - 1):
        second[k].wait_recv()
    finish(me, 2 * half - 1, in1.at[half - 1], in2)
    for k in range(half):
        first[k].wait_send()
    for k in range(half - 1):
        second[k].wait_send()


def grads_kernel(n, lanes, grads, basis, total, squares, whole, held, out1, in1, out2, in2, own_sq, in_sq, lane_sq, in_lane,
                 loads, s1, r1, s2, r2, sq_s, sq_r, lane_s, lane_r, b1, c1, b2, c2):
    half = n // 2
    rows, cols = total.shape
    strip = basis.shape[0]
    micro = held.shape[1]
    tile = 128
    me = lax.axis_index("fsdp")
    side = lax.rem(me, 2)
    pair = me // 2
    copies = []
    for k in range(half):
        group = lax.rem(pair + 1 + k, half)
        for which, chunk in ((0, 2 * group + 1 - side), (1, 2 * group + side)):
            start = pl.multiple_of(chunk * cols, 128)
            copies.append(pltpu.make_async_copy(
                grads.at[0, :, :, pl.ds(start, cols)], held.at[2 * k + which], loads.at[2 * k + which]))
    order = [0, 2] if half > 1 else [0]
    order += [i for i in range(n) if i not in order]
    for i in order:
        copies[i].start()
    greet(n, lanes)

    def local(slot, at):
        value = held[slot, 0, at, :].astype(f32)
        for index in range(1, micro):
            value = value + held[slot, index, at, :].astype(f32)
        return value

    def produce(chunk, slot, add, out):
        copies[slot].wait()

        def step(i, carry):
            at = pl.ds(pl.multiple_of(i * tile, tile), tile)
            value = local(slot, at)
            if add is not None:
                value = value + add[at, :].astype(f32)
            out[at, :] = value.astype(bf16)
            return carry

        lax.fori_loop(0, rows // tile, step, 0)

    def finish(chunk, slot, add, others):
        copies[slot].wait()

        def step(i, carry):
            at = pl.ds(pl.multiple_of(i * tile, tile), tile)
            value = local(slot, at) + add[at, :].astype(f32)
            for k in range(half - 1):
                value = value + others[k, at, :].astype(f32)
            total[at, :] = value.astype(bf16)
            return carry + jnp.sum((value * value).reshape(tile // 8, 8, cols), axis=0)

        sums = lax.fori_loop(0, rows // tile, step, jnp.zeros((8, cols), f32))
        part = sums[:, :128]
        for c in range(1, cols // 128):
            part = part + sums[:, c * 128 : (c + 1) * 128]
        own_sq[...] = part

    mate = me + 1 - 2 * side
    here = pl.ds(pl.multiple_of(me * strip, strip), strip)
    across = [remote(basis, whole.at[here], b2.at[k], c2.at[k], 2 * lax.rem(pair + 1 + k, half) + side)
              for k in range(half - 1)]
    near = []

    def beside(k):
        if k == 0:
            for copy in across:
                copy.start()
            near.append(remote(basis, whole.at[here], b1.at[0], c1.at[0], mate))
            whole[here, :] = basis[...]
        else:
            across[k - 1].wait_recv()
            source = 2 * lax.rem(pair + half - k, half) + side
            there = pl.ds(pl.multiple_of(source * strip, strip), strip)
            near.append(remote(whole.at[there], whole.at[there], b1.at[k], c1.at[k], mate))
        near[-1].start()

    exchange(n, produce, finish, out1, in1, out2, in2, s1, r1, s2, r2, beside)
    sends = [remote(own_sq, in_sq.at[k], sq_s.at[k], sq_r.at[k], lax.rem(me + 1 + k, n)) for k in range(n - 1)]
    for send in sends:
        send.start()
    value = own_sq[...]
    for k, send in enumerate(sends):
        send.wait()
        value = value + in_sq[k]
    lane_sq[...] = value
    lane = lax.axis_index("tp")
    sends = [remote(lane_sq, in_lane.at[k], lane_s.at[k], lane_r.at[k], lax.rem(lane + 1 + k, lanes), "tp")
             for k in range(lanes - 1)]
    for send in sends:
        send.start()
    for k, send in enumerate(sends):
        send.wait()
        value = value + in_lane[k]
    squares[...] = value
    for copy in near:
        copy.wait()
    for copy in across:
        copy.wait_send()


def sum_grads(grads, basis, n, lanes):
    unused, micro, rows, width = grads.shape
    cols = width // n
    half = n // 2
    dma = pltpu.SemaphoreType.DMA
    piece = pltpu.VMEM((half, rows, cols), bf16)
    small = max(half - 1, 1)
    other = pltpu.VMEM((small, rows, cols), bf16)
    return pl.pallas_call(
        functools.partial(grads_kernel, n, lanes),
        out_shape=(jax.ShapeDtypeStruct((rows, cols), bf16), jax.ShapeDtypeStruct((8, 128), f32),
                   jax.ShapeDtypeStruct((n * basis.shape[0], basis.shape[1]), bf16)),
        in_specs=[pl.BlockSpec(memory_space=pl.ANY), pl.BlockSpec(memory_space=pltpu.VMEM)],
        out_specs=(pl.BlockSpec(memory_space=pltpu.VMEM),) * 3,
        scratch_shapes=[
            pltpu.VMEM((n, micro, rows, cols), bf16), piece, piece, other, other,
            pltpu.VMEM((8, 128), f32), pltpu.VMEM((n - 1, 8, 128), f32),
            pltpu.VMEM((8, 128), f32), pltpu.VMEM((max(lanes - 1, 1), 8, 128), f32),
            dma((n,)), dma((half,)), dma((half,)), dma((small,)), dma((small,)),
            dma((n - 1,)), dma((n - 1,)), dma((max(lanes - 1, 1),)), dma((max(lanes - 1, 1),)),
            dma((half,)), dma((half,)), dma((small,)), dma((small,)),
        ],
        compiler_params=pltpu.CompilerParams(collective_id=0, has_side_effects=True, vmem_limit_bytes=57 * 1024 * 1024),
    )(grads, basis)


def outer_kernel(n, total, outer, out1, in1, out2, in2, s1, r1, s2, r2):
    half = n // 2
    strip = outer.shape[0]
    greet(n, 1)

    def local(chunk):
        at = pl.ds(pl.multiple_of(chunk * strip, strip), strip)
        return lax.dot_general(total[at, :], total[...], (((1,), (1,)), ((), ())), preferred_element_type=f32)

    def produce(chunk, slot, add, out):
        value = local(chunk)
        if add is not None:
            value = value + add[...].astype(f32)
        out[...] = value.astype(bf16)

    def finish(chunk, slot, add, others):
        value = local(chunk) + add[...].astype(f32)
        for k in range(half - 1):
            value = value + others[k].astype(f32)
        outer[...] = value

    exchange(n, produce, finish, out1, in1, out2, in2, s1, r1, s2, r2)


def sum_outer(total, n):
    rows = total.shape[0]
    strip = rows // n
    half = n // 2
    small = max(half - 1, 1)
    dma = pltpu.SemaphoreType.DMA
    piece = pltpu.VMEM((half, strip, rows), bf16)
    other = pltpu.VMEM((small, strip, rows), bf16)
    return pl.pallas_call(
        functools.partial(outer_kernel, n),
        out_shape=jax.ShapeDtypeStruct((strip, rows), f32),
        in_specs=[pl.BlockSpec(memory_space=pltpu.VMEM)],
        out_specs=pl.BlockSpec(memory_space=pltpu.VMEM),
        scratch_shapes=[piece, piece, other, other, dma((half,)), dma((half,)), dma((small,)), dma((small,))],
        compiler_params=pltpu.CompilerParams(collective_id=1, has_side_effects=True, vmem_limit_bytes=VMEM_BYTES),
    )(total)


def gather_kernel(n, own, every, s1, r1, s2, r2):
    half = n // 2
    me = lax.axis_index("fsdp")
    side = lax.rem(me, 2)
    pair = me // 2
    mate = me + 1 - 2 * side
    greet(n, 1)
    across = [remote(own, every.at[me], s2.at[k], r2.at[k], 2 * lax.rem(pair + 1 + k, half) + side)
              for k in range(half - 1)]
    for copy in across:
        copy.start()
    near = [remote(own, every.at[me], s1.at[0], r1.at[0], mate)]
    near[0].start()
    every[me] = own[...]
    for k in range(half - 1):
        across[k].wait_recv()
        source = 2 * lax.rem(pair + half - 1 - k, half) + side
        near.append(remote(every.at[source], every.at[source], s1.at[k + 1], r1.at[k + 1], mate))
        near[-1].start()
    for copy in near:
        copy.wait()
    for copy in across:
        copy.wait_send()


def gather_rows(own, n, key):
    strip, width = own.shape
    half = n // 2
    small = max(half - 1, 1)
    dma = pltpu.SemaphoreType.DMA
    every = pl.pallas_call(
        functools.partial(gather_kernel, n),
        out_shape=jax.ShapeDtypeStruct((n, strip, width), own.dtype),
        in_specs=[pl.BlockSpec(memory_space=pltpu.VMEM)],
        out_specs=pl.BlockSpec(memory_space=pltpu.VMEM),
        scratch_shapes=[dma((half,)), dma((half,)), dma((small,)), dma((small,))],
        compiler_params=pltpu.CompilerParams(collective_id=key, has_side_effects=True, vmem_limit_bytes=VMEM_BYTES),
    )(own)
    return every.reshape(n * strip, width)


SLICES = 4


def tail_kernel(n, power, own, weights, refreshed, every, gram, gram_low, bend, once, local,
                s1, r1, s2, r2, u1, v1, u2, v2):
    half = n // 2
    strip = power.shape[0]
    rows, cols = own.shape
    part = rows // SLICES
    block = 512
    me = lax.axis_index("fsdp")
    side = lax.rem(me, 2)
    pair = me // 2
    mate = me + 1 - 2 * side
    greet(n, 1)
    here = pl.ds(pl.multiple_of(me * strip, strip), strip)
    every[here, :] = power[...].astype(bf16)
    targets = [2 * lax.rem(pair + 1 + k, half) + side for k in range(half - 1)]
    sources = [2 * lax.rem(pair + half - 1 - k, half) + side for k in range(half - 1)]
    across = [remote(every.at[here], every.at[here], s2.at[k], r2.at[k], targets[k]) for k in range(half - 1)]
    near = [remote(every.at[here], every.at[here], s1.at[0], r1.at[0], mate)]
    for copy in across + near:
        copy.start()

    def window(device, piece):
        return weights.at[pl.ds(piece * part, part), pl.ds(pl.multiple_of(device * cols, 128), cols)]

    mine = pltpu.make_async_copy(own, weights.at[:, pl.ds(pl.multiple_of(me * cols, 128), cols)], local.at[0])
    mine.start()
    wide = []
    close = []

    def push(piece):
        for k in range(half - 1):
            wide.append(remote(own.at[pl.ds(piece * part, part)], window(me, piece),
                               u2.at[piece, k], v2.at[piece, k], targets[k]))
            wide[-1].start()
        close.append(remote(own.at[pl.ds(piece * part, part)], window(me, piece),
                            u1.at[piece, half - 1], v1.at[piece, half - 1], mate))
        close[-1].start()

    def relay(piece):
        for k in range(half - 1):
            wide[piece * (half - 1) + k].wait_recv()
            close.append(remote(window(sources[k], piece), window(sources[k], piece),
                                u1.at[piece, k], v1.at[piece, k], mate))
            close[-1].start()

    for k in range(half - 1):
        across[k].wait_recv()
        there = pl.ds(pl.multiple_of(sources[k] * strip, strip), strip)
        near.append(remote(every.at[there], every.at[there], s1.at[k + 1], r1.at[k + 1], mate))
        near[-1].start()
    push(0)
    push(1)
    for copy in near:
        copy.wait_recv()

    def sums(i, carry):
        value = every[pl.ds(pl.multiple_of(i * 128, 128), 128), :].astype(f32)
        return carry + jnp.sum((value * value).reshape(16, 8, rows), axis=0)

    total_sq = jnp.sum(lax.fori_loop(0, rows // 128, sums, jnp.zeros((8, rows), f32)), keepdims=True)
    norm = 1.0 / jnp.sqrt(total_sq + 1e-06)

    def blocks(step):
        def run(i, carry):
            step(pl.ds(pl.multiple_of(i * block, block), block))
            return carry

        lax.fori_loop(0, rows // block, run, 0)

    def make_gram(at):
        value = lax.dot_general(every[:, at], every[...], (((0,), (0,)), ((), ())), preferred_element_type=f32)
        value = value * (norm * norm)
        gram[at, :] = value
        gram_low[at, :] = value.astype(bf16)

    def make_bend(at):
        value = poly_second * gram[at, :] + poly_third * mm(gram_low[at, :], gram_low[...])
        bend[at, :] = value.astype(bf16)

    def make_once(at):
        value = poly_first * gram[at, :] + mm(bend[at, :], gram_low[...])
        gram[at, :] = value
        once[at, :] = value.astype(bf16)

    def make_second(at):
        value = poly_first * gram[at, :] + mm(bend[at, :], once[...])
        gram_low[at, :] = value.astype(bf16)

    blocks(make_gram)
    blocks(make_bend)
    relay(0)
    if SLICES > 2:
        push(2)
    blocks(make_once)
    blocks(make_second)
    current = power[...] * norm
    current = poly_first * current + mm(current, bend[...])
    product = mm(current, gram_low[...])
    refreshed[...] = poly_first * current + poly_second * product + poly_third * mm(product, gram_low[...])
    for piece in range(1, SLICES):
        relay(piece)
        if piece + 2 < SLICES:
            push(piece + 2)
    mine.wait()
    for copy in close:
        copy.wait()
    for copy in wide + near + across:
        copy.wait_send()


def finish_step(power, own, n):
    strip, width = power.shape
    rows, cols = own.shape
    half = n // 2
    small = max(half - 1, 1)
    dma = pltpu.SemaphoreType.DMA
    low = pltpu.VMEM((width, width), bf16)
    return pl.pallas_call(
        functools.partial(tail_kernel, n),
        out_shape=(jax.ShapeDtypeStruct((rows, n * cols), bf16), jax.ShapeDtypeStruct((strip, width), f32)),
        in_specs=[pl.BlockSpec(memory_space=pltpu.VMEM)] * 2,
        out_specs=(pl.BlockSpec(memory_space=pl.ANY), pl.BlockSpec(memory_space=pltpu.VMEM)),
        scratch_shapes=[low, pltpu.VMEM((width, width), f32), low, low, low, dma((1,)),
                        dma((half,)), dma((half,)), dma((small,)), dma((small,)),
                        dma((SLICES, half)), dma((SLICES, half)), dma((SLICES, small)), dma((SLICES, small))],
        compiler_params=pltpu.CompilerParams(collective_id=3, has_side_effects=True, vmem_limit_bytes=VMEM_BYTES),
    )(power, own)


def plain_grads(grads, n, lanes):
    rows = grads.shape[2]
    local = jnp.sum(grads.astype(f32), axis=(0, 1)).astype(bf16)
    pieces = lax.all_to_all(local, "fsdp", split_axis=1, concat_axis=0, tiled=True)
    summed = jnp.sum(pieces.reshape(n, rows, -1).astype(f32), axis=0)
    squares = lax.psum(jnp.sum(summed * summed), ("fsdp", "tp"))
    return summed.astype(bf16), squares


def body(n, lanes, grads, master, moment, second, stats, basis):
    rows, cols = master.shape
    own_rows = basis[0]
    stat_rows = stats[0]
    aligned = cols % 128 == 0 and n % 2 == 0
    if aligned:
        total, squares, whole = sum_grads(grads, own_rows.astype(bf16), n, lanes)
    else:
        whole = lax.all_gather(own_rows.astype(bf16), "fsdp", axis=0, tiled=True)
        total, squares = plain_grads(grads, n, lanes)
    ratio = jnp.minimum(1.0, jnp.sqrt(float(D * KVW) / (jnp.sum(squares) + 1e-06)))
    rotated = mm(whole.T, total) * ratio
    moment_new = 0.9 * moment + 0.1 * rotated
    second_new = 0.95 * second + 0.05 * rotated * rotated
    update = moment_new / (jnp.sqrt(second_new) + 1e-08)
    delta = mm(whole, update)
    master_new = master - 0.01 * (delta + 0.1 * master)
    outer = sum_outer(total, n) * (ratio * ratio)
    stats_new = 0.9 * stat_rows + 0.1 / KVW * outer
    top = stats_new.astype(bf16)
    power = mm(top, whole) + mm(stats_new - top.astype(f32), whole)
    if aligned:
        weights, current = finish_step(power, master_new.astype(bf16), n)
        return (weights, master_new, moment_new, second_new, stats_new[None], current[None])
    weights = lax.all_gather(master_new.astype(bf16), "fsdp", axis=1, tiled=True)
    every = gather_rows(power.astype(bf16), n, 2)
    raw = mm(every.T, every)
    norm = 1.0 / jnp.sqrt(jnp.sum(jnp.square(every.astype(f32))) + 1e-06)
    gram = raw * (norm * norm)
    current = power * norm
    bend = poly_second * gram + poly_third * mm(gram, gram)
    current = poly_first * current + mm(current, bend)
    once = poly_first * gram + mm(bend, gram)
    gram = poly_first * once + mm(bend, once)
    product = mm(current, gram)
    current = poly_first * current + poly_second * product + poly_third * mm(product, gram)
    return (weights, master_new, moment_new, second_new, stats_new[None], current[None])


def solution(mesh):
    in_specs = (
        P("fsdp", None, "tp", None),
        P("tp", "fsdp"),
        P("tp", "fsdp"),
        P("tp", "fsdp"),
        P("tp", "fsdp", None),
        P("tp", "fsdp", None),
    )
    out_specs = (
        P("tp", None),
        P("tp", "fsdp"),
        P("tp", "fsdp"),
        P("tp", "fsdp"),
        P("tp", "fsdp", None),
        P("tp", "fsdp", None),
    )
    step = functools.partial(body, mesh.shape["fsdp"], mesh.shape["tp"])
    return jax.shard_map(step, mesh=mesh, in_specs=in_specs, out_specs=out_specs, check_vma=False)
```
